32 devices in a mesh: layer: 4 (over y, x), row: 2 (over core), col: 4 (over z).
Axes of the slice: x: 2, y: 2, z: 4, core: 2. Of those that a mesh axis runs over, the one named last changes fastest.
Arguments:
- blocks: bfloat16 [13, 512, 128, 128], P(None, ('row', 'col'), 'layer'), may hold values from -0.29882812 to 0.29882812
- presence: int32 [13, 512], P(None, ('row', 'col')), may hold values from 0 to 1, as said below
Outputs:
- purified: bfloat16 [13, 512, 128, 128], P(None, ('row', 'col'), 'layer')
The draws below stay inside these ranges and needn't reach their ends.
Inputs may be any that keep to these rules, and one draw needn't show every extreme that they name: `presence`: the tile on offset 0 is present in every block row.
All inputs are finite; a program needn't handle non-finite values.
Results may differ from the reference program's by a relative error of at most 0.01.
Values may be sent and summed in bfloat16 or wider, within the bound.
A program may use at most 320 MiB of HBM per device.

```python
import jax
import jax.numpy as jnp

BS = 128
NBG = 512
BAND = 3
FAR = 160
DIAGS = 13


def draw_presence(key, part):
    key_band, key_level, key_far = jax.random.split(key, 3)
    band_rows = (jax.random.randint(key_band, (2 * BAND + 1, NBG), 0, 8) < 7).astype(jnp.int32)
    band_rows = band_rows.at[BAND].set(1)
    levels = jax.random.randint(key_level, (NBG // 8,), 1, 8)
    levels = jnp.repeat(levels, 8)
    far_rows = (jax.random.randint(key_far, (6, NBG), 0, 8) < levels[None, :]).astype(jnp.int32)
    return jnp.concatenate([band_rows, far_rows], axis=0).astype(jnp.int32)


def block_levels(key, shape, cuts, smallest, high):
    def one(position, shards_of):
        heights = jax.random.uniform(jax.random.fold_in(jax.random.fold_in(key, 6), position), (shards_of,), jnp.float32, smallest / len(cuts), high / len(cuts))
        return jnp.repeat(jnp.exp(heights), shape[position] // shards_of).reshape((-1,) + (1,) * (len(shape) - position - 1))

    factor_of = one(*cuts[0])
    for cut in cuts[1:]:
        factor_of = factor_of * one(*cut)
    return factor_of


def normal_values(key, shape, width, limit, cuts=(), held_as=jnp.bfloat16):
    result = width * jax.random.normal(key, shape, jnp.float32)
    if cuts:
        result = result * block_levels(key, shape, cuts, -0.22, 0.18)
    return jnp.clip(result, -limit, limit).astype(held_as)


def setup_inputs(seed: int = 0) -> dict:
    keys = jax.random.split(jax.random.key(seed), 3)
    blocks = normal_values(keys[0], (DIAGS, NBG, BS, BS), 0.05, 0.29882812, ((1, 8), (2, 4)))
    presence = draw_presence(jax.random.fold_in(keys[2], 71), 0)
    return {"blocks": blocks, "presence": presence}


def offset_table():
    values = list(range(-BAND, BAND + 1))
    values = values + [FAR - 1, FAR, FAR + 1, -FAR - 1, -FAR, -FAR + 1]
    return [value % NBG for value in values]


def pair_table(offsets):
    by_target = []
    for target_index in range(len(offsets)):
        entries = []
        for left_index in range(len(offsets)):
            for right_index in range(len(offsets)):
                if (offsets[left_index] + offsets[right_index]) % NBG == offsets[target_index]:
                    entries.append((left_index, right_index))
        by_target.append(entries)
    return by_target


def reference(blocks, presence):
    offsets = offset_table()
    by_target = pair_table(offsets)
    weight_mask = presence.astype(jnp.float32)[:, :, None, None]
    masked = blocks * presence.astype(jnp.bfloat16)[:, :, None, None]

    def product(left_tiles):
        totals = []
        for target_index in range(len(offsets)):
            total = jnp.zeros((NBG, BS, BS), jnp.float32)
            for left_index, right_index in by_target[target_index]:
                moved = jnp.roll(masked[right_index], -offsets[left_index], axis=0)
                total = total + jnp.einsum("ixz,izy->ixy", left_tiles[left_index].astype(jnp.float32), moved.astype(jnp.float32))
            totals.append(total)
        return jnp.stack(totals) * weight_mask

    second = product(masked).astype(jnp.bfloat16)
    third = product(second)
    return (3.0 * second.astype(jnp.float32) - 2.0 * third).astype(jnp.bfloat16)
```

```python
import functools

import jax
import jax.numpy as jnp
from jax import lax
from jax.experimental import pallas as pl
from jax.experimental.pallas import tpu as pltpu
from jax.sharding import PartitionSpec as P

BAND = 3
FAR = 160
WIDTH = 2 * BAND + 1
MESH = pl.DeviceIdType.MESH


def offset_table(total_rows):
    values = list(range(-BAND, BAND + 1))
    values = values + [FAR - 1, FAR, FAR + 1, -FAR - 1, -FAR, -FAR + 1]
    return [value % total_rows for value in values]


def pair_table(offsets, total_rows):
    by_target = []
    for target in offsets:
        entries = []
        for left_index, left in enumerate(offsets):
            for right_index, right in enumerate(offsets):
                if (left + right) % total_rows == target:
                    entries.append((left_index, right_index))
        by_target.append(entries)
    return by_target


def runs_of(indices):
    runs = []
    for position, index in enumerate(indices):
        if runs and runs[-1][1] + runs[-1][2] == index:
            runs[-1][2] += 1
        else:
            runs.append([position, index, 1])
    return runs


def pieces_of(low, high, local_rows):
    for ahead in range(low // local_rows, (high - 1) // local_rows + 1):
        first = max(low, ahead * local_rows)
        last = min(high, (ahead + 1) * local_rows)
        yield ahead, first - ahead * local_rows, last - first, first - low


def kernel(sizes, needed, by_target, tiles, presence, out, near, ahead_far, behind_far, squared, done,
           send_sem, near_sem, ahead_sem, behind_sem, out_send_sem, out_sem):
    groups, columns, layers, local_rows, rows, part, size = sizes
    me_layer = lax.axis_index("layer")
    me_group = lax.axis_index("row") * columns + lax.axis_index("col")

    def device(steps, layer):
        group = lax.rem(me_group + steps % groups, groups)
        return {"row": lax.div(group, columns), "col": lax.rem(group, columns), "layer": layer}

    everything = list(range(len(by_target)))
    windows = [
        (near, near_sem, -BAND, rows + BAND, everything),
        (ahead_far, ahead_sem, FAR - 1, rows + FAR + 1, needed[0]),
        (behind_far, behind_sem, -FAR - 1, rows - FAR + 1, needed[1]),
    ]
    my_part = pl.ds(pl.multiple_of(me_layer * part, part), part)

    def each_copy(act_remote, act_local):
        for window, sem, low, high, diagonals in windows:
            for layer in range(layers):
                for steps, source_row, count, window_row in pieces_of(
                    low + layer * rows, high + layer * rows, local_rows
                ):
                    for position, index, length in runs_of(diagonals):
                        source = tiles.at[pl.ds(index, length), pl.ds(source_row, count)]
                        target = window.at[pl.ds(position, length), pl.ds(window_row, count), my_part]

                        def remote():
                            act_remote(
                                pltpu.make_async_remote_copy(
                                    src_ref=source, dst_ref=target, send_sem=send_sem, recv_sem=sem,
                                    device_id=device(-steps, layer), device_id_type=MESH,
                                )
                            )

                        def local():
                            if act_local is not None:
                                act_local(pltpu.make_async_copy(source, target, sem))

                        if steps % groups == 0:
                            pl.when(me_layer != layer)(remote)
                            pl.when(me_layer == layer)(local)
                        else:
                            remote()

    each_copy(lambda copy: copy.start(), lambda copy: copy.start())
    each_copy(lambda copy: copy.wait_send(), None)
    for window, sem, *_ in windows:
        pltpu.make_async_copy(window, window, sem).wait()

    def right_tile(left, right, row):
        if left < WIDTH:
            return near[right, row + left]
        if left < WIDTH + 3:
            return ahead_far[needed[0].index(right), row + left - WIDTH]
        return behind_far[needed[1].index(right), row + left - WIDTH - 3]

    couples = [(0, 1), (2, 3), (4, 5), (6,), (7, 8), (9,), (10, 11), (12,)]

    def product(left_tile, row, finish):
        for couple in couples:
            tables = [dict(by_target[target]) for target in couple]
            lefts = sorted(set(left for table in tables for left in table))
            lhs = jnp.concatenate([left_tile(left) for left in lefts], axis=1)
            rhs = jnp.concatenate(
                [
                    jnp.concatenate(
                        [
                            right_tile(left, table[left], row)
                            if left in table
                            else jnp.zeros((size, size), jnp.bfloat16)
                            for table in tables
                        ],
                        axis=1,
                    )
                    for left in lefts
                ],
                axis=0,
            )
            total = jnp.dot(lhs, rhs, preferred_element_type=jnp.float32)
            for place, target in enumerate(couple):
                finish(target, total[:, place * size : (place + 1) * size])

    def each_result(row, act_remote, act_local):
        place = me_layer * rows + row
        for layer in range(layers):
            source = done.at[row, :, pl.ds(layer * part, part)]
            target = out.at[:, place]

            def remote():
                act_remote(
                    pltpu.make_async_remote_copy(
                        src_ref=source, dst_ref=target, send_sem=out_send_sem, recv_sem=out_sem,
                        device_id=device(0, layer), device_id_type=MESH,
                    )
                )

            def local():
                if act_local is not None:
                    act_local(pltpu.make_async_copy(source, target, out_sem))

            pl.when(me_layer != layer)(remote)
            pl.when(me_layer == layer)(local)

    def start(copy):
        copy.start()

    @pl.loop(0, rows)
    def _(row):
        def weight(target):
            return presence[target, me_layer * rows + row].astype(jnp.float32)

        def store_square(target, total):
            squared[target] = (total * weight(target)).astype(jnp.bfloat16)

        def store_result(target, total):
            third = total * weight(target)
            done[row, target] = (3.0 * squared[target].astype(jnp.float32) - 2.0 * third).astype(jnp.bfloat16)

        product(lambda left: near[left, row + BAND], row, store_square)
        product(lambda left: squared[left], row, store_result)

        @pl.when(row > 0)
        def _():
            each_result(row - 1, start, start)

    each_result(rows - 1, start, start)

    @pl.loop(0, rows)
    def _(row):
        each_result(row, lambda copy: copy.wait_send(), None)

    pltpu.make_async_copy(out, out, out_sem).wait()


def solution(mesh):
    columns = mesh.shape["col"]
    layers = mesh.shape["layer"]
    groups = mesh.shape["row"] * columns

    def per_device(blocks, presence):
        diagonals, local_rows, part, size = blocks.shape
        total_rows = local_rows * groups
        rows = local_rows // layers
        offsets = offset_table(total_rows)
        by_target = pair_table(offsets, total_rows)
        needed = []
        for first in (WIDTH, WIDTH + 3):
            lefts = range(first, first + 3)
            needed.append(sorted(set(b for pairs in by_target for a, b in pairs if a in lefts)))
        masked = blocks * presence.astype(jnp.bfloat16)[:, :, None, None]
        sizes = (groups, columns, layers, local_rows, rows, part, size)
        return pl.pallas_call(
            functools.partial(kernel, sizes, needed, by_target),
            out_shape=jax.ShapeDtypeStruct(blocks.shape, jnp.bfloat16),
            in_specs=[pl.BlockSpec(memory_space=pl.ANY), pl.BlockSpec(memory_space=pltpu.SMEM)],
            out_specs=pl.BlockSpec(memory_space=pl.ANY),
            scratch_shapes=[
                pltpu.VMEM((diagonals, rows + 2 * BAND, size, size), jnp.bfloat16),
                pltpu.VMEM((len(needed[0]), rows + 2, size, size), jnp.bfloat16),
                pltpu.VMEM((len(needed[1]), rows + 2, size, size), jnp.bfloat16),
                pltpu.VMEM((diagonals, size, size), jnp.bfloat16),
                pltpu.VMEM((rows, diagonals, size, size), jnp.bfloat16),
            ]
            + [pltpu.SemaphoreType.DMA] * 6,
            compiler_params=pltpu.CompilerParams(has_side_effects=True, vmem_limit_bytes=48 * 2**20),
        )(masked, presence)

    return jax.shard_map(
        per_device,
        mesh=mesh,
        in_specs=(P(None, ("row", "col"), "layer", None), P(None, ("row", "col"))),
        out_specs=P(None, ("row", "col"), "layer", None),
        check_vma=False,
    )
```

```python
import functools

import jax
import jax.numpy as jnp
from jax import lax
from jax.experimental import pallas as pl
from jax.experimental.pallas import tpu as pltpu
from jax.sharding import PartitionSpec as P

BAND = 3
FAR = 160
CHUNKS = 4
WIDTH = 2 * BAND + 1
MESH = pl.DeviceIdType.MESH


def offset_table(total_rows):
    values = list(range(-BAND, BAND + 1))
    values = values + [FAR - 1, FAR, FAR + 1, -FAR - 1, -FAR, -FAR + 1]
    return [value % total_rows for value in values]


def pair_table(offsets, total_rows):
    by_target = []
    for target in offsets:
        entries = []
        for left_index, left in enumerate(offsets):
            for right_index, right in enumerate(offsets):
                if (left + right) % total_rows == target:
                    entries.append((left_index, right_index))
        by_target.append(entries)
    return by_target


def runs_of(indices):
    runs = []
    for position, index in enumerate(indices):
        if runs and runs[-1][1] + runs[-1][2] == index:
            runs[-1][2] += 1
        else:
            runs.append([position, index, 1])
    return runs


def pieces_of(low, high, local_rows):
    for ahead in range(low // local_rows, (high - 1) // local_rows + 1):
        first = max(low, ahead * local_rows)
        last = min(high, (ahead + 1) * local_rows)
        yield ahead, first - ahead * local_rows, last - first, first - low


def kernel(sizes, needed, by_target, tiles, presence, out, near, ahead_far, behind_far, squared, done,
           send_sem, near_sem, ahead_sem, behind_sem, out_send_sem, out_sem):
    groups, columns, layers, local_rows, rows, part, size = sizes
    me_layer = lax.axis_index("layer")
    me_group = lax.axis_index("row") * columns + lax.axis_index("col")

    def device(steps, layer):
        group = lax.rem(me_group + steps % groups, groups)
        return {"row": lax.div(group, columns), "col": lax.rem(group, columns), "layer": layer}

    everything = list(range(len(by_target)))
    windows = [
        (near, near_sem, -BAND, 2 * BAND, everything),
        (ahead_far, ahead_sem, FAR - 1, 2, needed[0]),
        (behind_far, behind_sem, -FAR - 1, 2, needed[1]),
    ]
    chunks = CHUNKS if rows % CHUNKS == 0 else rows
    step_rows = rows // chunks

    def chunk_rows(chunk, extra):
        first = 0 if chunk == 0 else chunk * step_rows + extra
        return first, (chunk + 1) * step_rows + extra

    def copies_to(chunk, layer, act_remote, act_local):
        for window, sem, low, extra, diagonals in windows:
            first, last = chunk_rows(chunk, extra)
            start_row = low + layer * rows
            for steps, source_row, count, window_row in pieces_of(
                start_row + first, start_row + last, local_rows
            ):
                for position, index, length in runs_of(diagonals):
                    source = tiles.at[pl.ds(index, length), pl.ds(source_row, count)]
                    target = window.at[me_layer, pl.ds(position, length), pl.ds(first + window_row, count)]

                    def remote():
                        act_remote(
                            pltpu.make_async_remote_copy(
                                src_ref=source, dst_ref=target, send_sem=send_sem, recv_sem=sem.at[chunk],
                                device_id=device(-steps, layer), device_id_type=MESH,
                            )
                        )

                    def local():
                        if act_local is not None:
                            act_local(pltpu.make_async_copy(source, target, sem.at[chunk]))

                    if steps % groups == 0:
                        pl.when(me_layer != layer)(remote)
                        pl.when(me_layer == layer)(local)
                    else:
                        remote()

    def start(copy):
        copy.start()

    for chunk in range(chunks):
        for turn in range(layers):
            for layer in range(layers):

                @pl.when(lax.rem(me_layer + turn, layers) == layer)
                def _():
                    copies_to(chunk, layer, start, start)

    def wait_for(chunk):
        for window, sem, _, extra, _ in windows:
            first, last = chunk_rows(chunk, extra)
            arrived = window.at[:, :, pl.ds(first, last - first)]
            pltpu.make_async_copy(arrived, arrived, sem.at[chunk]).wait()

    def tile_of(window, index, row):
        return jnp.concatenate([window[layer, index, row] for layer in range(layers)], axis=0)

    def right_tile(left, right, row):
        if left < WIDTH:
            return tile_of(near, right, row + left)
        if left < WIDTH + 3:
            return tile_of(ahead_far, needed[0].index(right), row + left - WIDTH)
        return tile_of(behind_far, needed[1].index(right), row + left - WIDTH - 3)

    couples = [(0, 1), (2, 3), (4, 5), (6,), (7, 8), (9,), (10, 11), (12,)]

    def product(left_tile, row, finish):
        for couple in couples:
            tables = [dict(by_target[target]) for target in couple]
            lefts = sorted(set(left for table in tables for left in table))
            lhs = jnp.concatenate([left_tile(left) for left in lefts], axis=1)
            rhs = jnp.concatenate(
                [
                    jnp.concatenate(
                        [
                            right_tile(left, table[left], row)
                            if left in table
                            else jnp.zeros((size, size), jnp.bfloat16)
                            for table in tables
                        ],
                        axis=1,
                    )
                    for left in lefts
                ],
                axis=0,
            )
            total = jnp.dot(lhs, rhs, preferred_element_type=jnp.float32)
            for place, target in enumerate(couple):
                finish(target, total[:, place * size : (place + 1) * size])

    def each_result(row, act_remote, act_local):
        place = me_layer * rows + row
        for layer in range(layers):
            source = done.at[row, layer]
            target = out.at[:, place]

            def remote():
                act_remote(
                    pltpu.make_async_remote_copy(
                        src_ref=source, dst_ref=target, send_sem=out_send_sem, recv_sem=out_sem,
                        device_id=device(0, layer), device_id_type=MESH,
                    )
                )

            def local():
                if act_local is not None:
                    act_local(pltpu.make_async_copy(source, target, out_sem))

            pl.when(me_layer != layer)(remote)
            pl.when(me_layer == layer)(local)

    @pl.loop(0, rows)
    def _(row):
        for chunk in range(chunks):

            @pl.when(row == chunk * step_rows)
            def _():
                wait_for(chunk)

        def weight(target):
            return presence[target, me_layer * rows + row].astype(jnp.float32)

        def store_square(target, total):
            squared[target] = (total * weight(target)).astype(jnp.bfloat16)

        def store_result(target, total):
            third = total * weight(target)
            result = (3.0 * squared[target].astype(jnp.float32) - 2.0 * third).astype(jnp.bfloat16)
            for layer in range(layers):
                done[row, layer, target] = result[layer * part : (layer + 1) * part]

        product(lambda left: tile_of(near, left, row + BAND), row, store_square)
        product(lambda left: squared[left], row, store_result)

        @pl.when(row > 0)
        def _():
            each_result(row - 1, start, start)

    each_result(rows - 1, start, start)
    for chunk in range(chunks):
        for layer in range(layers):
            copies_to(chunk, layer, lambda copy: copy.wait_send(), None)

    @pl.loop(0, rows)
    def _(row):
        each_result(row, lambda copy: copy.wait_send(), None)

    pltpu.make_async_copy(out, out, out_sem).wait()


def solution(mesh):
    columns = mesh.shape["col"]
    layers = mesh.shape["layer"]
    groups = mesh.shape["row"] * columns

    def per_device(blocks, presence):
        diagonals, local_rows, part, size = blocks.shape
        total_rows = local_rows * groups
        rows = local_rows // layers
        offsets = offset_table(total_rows)
        by_target = pair_table(offsets, total_rows)
        needed = []
        for first in (WIDTH, WIDTH + 3):
            lefts = range(first, first + 3)
            needed.append(sorted(set(b for pairs in by_target for a, b in pairs if a in lefts)))
        masked = blocks * presence.astype(jnp.bfloat16)[:, :, None, None]
        sizes = (groups, columns, layers, local_rows, rows, part, size)
        return pl.pallas_call(
            functools.partial(kernel, sizes, needed, by_target),
            out_shape=jax.ShapeDtypeStruct(blocks.shape, jnp.bfloat16),
            in_specs=[pl.BlockSpec(memory_space=pl.ANY), pl.BlockSpec(memory_space=pltpu.SMEM)],
            out_specs=pl.BlockSpec(memory_space=pl.ANY),
            scratch_shapes=[
                pltpu.VMEM((layers, diagonals, rows + 2 * BAND, part, size), jnp.bfloat16),
                pltpu.VMEM((layers, len(needed[0]), rows + 2, part, size), jnp.bfloat16),
                pltpu.VMEM((layers, len(needed[1]), rows + 2, part, size), jnp.bfloat16),
                pltpu.VMEM((diagonals, size, size), jnp.bfloat16),
                pltpu.VMEM((rows, layers, diagonals, part, size), jnp.bfloat16),
                pltpu.SemaphoreType.DMA,
                pltpu.SemaphoreType.DMA((rows,)),
                pltpu.SemaphoreType.DMA((rows,)),
                pltpu.SemaphoreType.DMA((rows,)),
                pltpu.SemaphoreType.DMA,
                pltpu.SemaphoreType.DMA,
            ],
            compiler_params=pltpu.CompilerParams(has_side_effects=True, vmem_limit_bytes=48 * 2**20),
        )(masked, presence)

    return jax.shard_map(
        per_device,
        mesh=mesh,
        in_specs=(P(None, ("row", "col"), "layer", None), P(None, ("row", "col"))),
        out_specs=P(None, ("row", "col"), "layer", None),
        check_vma=False,
    )
```

```python
import functools

import jax
import jax.numpy as jnp
from jax import lax
from jax.experimental import pallas as pl
from jax.experimental.pallas import tpu as pltpu
from jax.sharding import PartitionSpec as P

BAND = 3
FAR = 160
CHUNKS = 8
WIDTH = 2 * BAND + 1
MESH = pl.DeviceIdType.MESH


def offset_table(total_rows):
    values = list(range(-BAND, BAND + 1))
    values = values + [FAR - 1, FAR, FAR + 1, -FAR - 1, -FAR, -FAR + 1]
    return [value % total_rows for value in values]


def pair_table(offsets, total_rows):
    by_target = []
    for target in offsets:
        entries = []
        for left_index, left in enumerate(offsets):
            for right_index, right in enumerate(offsets):
                if (left + right) % total_rows == target:
                    entries.append((left_index, right_index))
        by_target.append(entries)
    return by_target


def runs_of(indices):
    runs = []
    for position, index in enumerate(indices):
        if runs and runs[-1][1] + runs[-1][2] == index:
            runs[-1][2] += 1
        else:
            runs.append([position, index, 1])
    return runs


def pieces_of(low, high, local_rows):
    for ahead in range(low // local_rows, (high - 1) // local_rows + 1):
        first = max(low, ahead * local_rows)
        last = min(high, (ahead + 1) * local_rows)
        yield ahead, first - ahead * local_rows, last - first, first - low


def kernel(sizes, needed, by_target, tiles, presence, out, near, ahead_far, behind_far, squared, done,
           send_sem, near_sem, ahead_sem, behind_sem, out_send_sem, out_sem):
    groups, columns, layers, local_rows, rows, part, size = sizes
    me_layer = lax.axis_index("layer")
    me_group = lax.axis_index("row") * columns + lax.axis_index("col")

    def device(steps, layer):
        group = lax.rem(me_group + steps % groups, groups)
        return {"row": lax.div(group, columns), "col": lax.rem(group, columns), "layer": layer}

    everything = list(range(len(by_target)))
    windows = [
        (near, near_sem, -BAND, 2 * BAND, everything),
        (ahead_far, ahead_sem, FAR - 1, 2, needed[0]),
        (behind_far, behind_sem, -FAR - 1, 2, needed[1]),
    ]
    chunks = CHUNKS if rows % CHUNKS == 0 else rows
    step_rows = rows // chunks

    def chunk_rows(chunk, extra):
        first = 0 if chunk == 0 else chunk * step_rows + extra
        return first, (chunk + 1) * step_rows + extra

    def copies_to(chunk, layer, act_remote, act_local):
        for window, sem, low, extra, diagonals in windows:
            first, last = chunk_rows(chunk, extra)
            start_row = low + layer * rows
            for steps, source_row, count, window_row in pieces_of(
                start_row + first, start_row + last, local_rows
            ):
                for position, index, length in runs_of(diagonals):
                    source = tiles.at[pl.ds(index, length), pl.ds(source_row, count)]
                    target = window.at[me_layer, pl.ds(position, length), pl.ds(first + window_row, count)]

                    def remote():
                        act_remote(
                            pltpu.make_async_remote_copy(
                                src_ref=source, dst_ref=target, send_sem=send_sem, recv_sem=sem.at[chunk],
                                device_id=device(-steps, layer), device_id_type=MESH,
                            )
                        )

                    def local():
                        if act_local is not None:
                            act_local(pltpu.make_async_copy(source, target, sem.at[chunk]))

                    if steps % groups == 0:
                        pl.when(me_layer != layer)(remote)
                        pl.when(me_layer == layer)(local)
                    else:
                        remote()

    def start(copy):
        copy.start()

    for chunk in range(chunks):
        for turn in range(layers):
            for layer in range(layers):

                @pl.when(lax.rem(me_layer + turn, layers) == layer)
                def _():
                    copies_to(chunk, layer, start, start)

    def wait_for(chunk):
        for window, sem, _, extra, _ in windows:
            first, last = chunk_rows(chunk, extra)
            arrived = window.at[:, :, pl.ds(first, last - first)]
            pltpu.make_async_copy(arrived, arrived, sem.at[chunk]).wait()

    def tile_of(window, index, row):
        return jnp.concatenate([window[layer, index, row] for layer in range(layers)], axis=0)

    def right_tile(left, right, row):
        if left < WIDTH:
            return tile_of(near, right, row + left)
        if left < WIDTH + 3:
            return tile_of(ahead_far, needed[0].index(right), row + left - WIDTH)
        return tile_of(behind_far, needed[1].index(right), row + left - WIDTH - 3)

    couples = [(0, 1), (2, 3), (4, 5), (6,), (7, 8), (9,), (10, 11), (12,)]

    def product(left_tile, row, finish):
        for couple in couples:
            tables = [dict(by_target[target]) for target in couple]
            lefts = sorted(set(left for table in tables for left in table))
            lhs = jnp.concatenate([left_tile(left) for left in lefts], axis=1)
            rhs = jnp.concatenate(
                [
                    jnp.concatenate(
                        [
                            right_tile(left, table[left], row)
                            if left in table
                            else jnp.zeros((size, size), jnp.bfloat16)
                            for table in tables
                        ],
                        axis=1,
                    )
                    for left in lefts
                ],
                axis=0,
            )
            total = jnp.dot(lhs, rhs, preferred_element_type=jnp.float32)
            for place, target in enumerate(couple):
                finish(target, total[:, place * size : (place + 1) * size])

    def each_result(row, act_remote, act_local):
        place = me_layer * rows + row
        for layer in range(layers):
            source = done.at[row, layer]
            target = out.at[:, place]

            def remote():
                act_remote(
                    pltpu.make_async_remote_copy(
                        src_ref=source, dst_ref=target, send_sem=out_send_sem, recv_sem=out_sem,
                        device_id=device(0, layer), device_id_type=MESH,
                    )
                )

            def local():
                if act_local is not None:
                    act_local(pltpu.make_async_copy(source, target, out_sem))

            pl.when(me_layer != layer)(remote)
            pl.when(me_layer == layer)(local)

    @pl.loop(0, rows)
    def _(row):
        for chunk in range(chunks):

            @pl.when(row == chunk * step_rows)
            def _():
                wait_for(chunk)

        def weight(target):
            return presence[target, me_layer * rows + row].astype(jnp.float32)

        def store_square(target, total):
            squared[target] = (total * weight(target)).astype(jnp.bfloat16)

        def store_result(target, total):
            third = total * weight(target)
            result = (3.0 * squared[target].astype(jnp.float32) - 2.0 * third).astype(jnp.bfloat16)
            for layer in range(layers):
                done[row, layer, target] = result[layer * part : (layer + 1) * part]

        product(lambda left: tile_of(near, left, row + BAND), row, store_square)
        product(lambda left: squared[left], row, store_result)

        @pl.when(row > 0)
        def _():
            each_result(row - 1, start, start)

    each_result(rows - 1, start, start)
    for chunk in range(chunks):
        for layer in range(layers):
            copies_to(chunk, layer, lambda copy: copy.wait_send(), None)

    @pl.loop(0, rows)
    def _(row):
        each_result(row, lambda copy: copy.wait_send(), None)

    pltpu.make_async_copy(out, out, out_sem).wait()


def solution(mesh):
    columns = mesh.shape["col"]
    layers = mesh.shape["layer"]
    groups = mesh.shape["row"] * columns

    def per_device(blocks, presence):
        diagonals, local_rows, part, size = blocks.shape
        total_rows = local_rows * groups
        rows = local_rows // layers
        offsets = offset_table(total_rows)
        by_target = pair_table(offsets, total_rows)
        needed = []
        for first in (WIDTH, WIDTH + 3):
            lefts = range(first, first + 3)
            needed.append(sorted(set(b for pairs in by_target for a, b in pairs if a in lefts)))
        masked = blocks * presence.astype(jnp.bfloat16)[:, :, None, None]
        sizes = (groups, columns, layers, local_rows, rows, part, size)
        return pl.pallas_call(
            functools.partial(kernel, sizes, needed, by_target),
            out_shape=jax.ShapeDtypeStruct(blocks.shape, jnp.bfloat16),
            in_specs=[pl.BlockSpec(memory_space=pl.ANY), pl.BlockSpec(memory_space=pltpu.SMEM)],
            out_specs=pl.BlockSpec(memory_space=pl.ANY),
            scratch_shapes=[
                pltpu.VMEM((layers, diagonals, rows + 2 * BAND, part, size), jnp.bfloat16),
                pltpu.VMEM((layers, len(needed[0]), rows + 2, part, size), jnp.bfloat16),
                pltpu.VMEM((layers, len(needed[1]), rows + 2, part, size), jnp.bfloat16),
                pltpu.VMEM((diagonals, size, size), jnp.bfloat16),
                pltpu.VMEM((rows, layers, diagonals, part, size), jnp.bfloat16),
                pltpu.SemaphoreType.DMA,
                pltpu.SemaphoreType.DMA((rows,)),
                pltpu.SemaphoreType.DMA((rows,)),
                pltpu.SemaphoreType.DMA((rows,)),
                pltpu.SemaphoreType.DMA,
                pltpu.SemaphoreType.DMA,
            ],
            compiler_params=pltpu.CompilerParams(has_side_effects=True, vmem_limit_bytes=48 * 2**20),
        )(masked, presence)

    return jax.shard_map(
        per_device,
        mesh=mesh,
        in_specs=(P(None, ("row", "col"), "layer", None), P(None, ("row", "col"))),
        out_specs=P(None, ("row", "col"), "layer", None),
        check_vma=False,
    )
```
